32 devices in a mesh: band: 4 (over y, x), pulse: 2 (over core), range: 4 (over z).
Axes of the slice: x: 2, y: 2, z: 4, core: 2. Of those that a mesh axis runs over, the one named last changes fastest.
Arguments:
- echoes: bfloat16 [4, 2, 8192, 4096], P('band', None, 'pulse', 'range'), may hold values from -6 to 6
- range_phase: float32 [4, 4096], P('band'), may hold values from -3.140625 to 3.140625
- pulse_shift: int32 [4, 8192], P('band', ('pulse', 'range')), may hold values from -64 to 64
- bin_offset: int32 [4], replicated, may hold values from 0 to 1024, as said below
- doppler_phase: float32 [8192], replicated, may hold values from -3.140625 to 3.140625
Outputs:
- focused: bfloat16 [12288, 2, 8192], P(('band', 'pulse', 'range'))
The draws below stay inside these ranges and needn't reach their ends.
Inputs may be any that keep to these rules, and one draw needn't show every extreme that they name: Band b's spectrum begins at combined bin b * 3072 - 2 * 512 + bin_offset[b]. In every draw some band other than the last has offset 2 * 512 and the band after it has offset 0.
All inputs are finite; a program needn't handle non-finite values.
Results may differ from the reference program's by a relative error of at most 0.0054.
Values may be sent and summed in bfloat16 or wider, within the bound.
A program may use at most 192 MiB of HBM per device.

```python
import math
import jax
import jax.numpy as jnp
from jax import lax

PULSES = 8192
CELLS = 4096
MARGIN = 512
SHIFT_MAX = 64
BANDS = 4
OWNED = 3072
COMBINED = 12288


def draw_bin_offset(key, part):
    key_draw, key_pick = jax.random.split(jax.random.fold_in(key, 17))
    offsets = jax.random.randint(key_draw, (BANDS,), 0, 2 * MARGIN + 1)
    chosen = jax.random.randint(key_pick, (), 0, BANDS - 1)
    position = jnp.arange(BANDS)
    offsets = jnp.where(position == chosen, 2 * MARGIN, offsets)
    offsets = jnp.where(position == chosen + 1, 0, offsets)
    return offsets.astype(jnp.int32)


def place_ends(entries, key, least, largest):
    shape = entries.shape
    place = [jax.random.randint(jax.random.fold_in(key, axis), (), 0, shape[axis]) for axis in range(len(shape))]
    entries = entries.at[tuple(place)].set(least)
    longest = shape.index(max(shape))
    place[longest] = (place[longest] + 1) % shape[longest]
    return entries.at[tuple(place)].set(largest)


def steps_of(stream_key, shape, pieces, least, high):
    def one(dim, blocks):
        draws = jax.random.uniform(jax.random.fold_in(jax.random.fold_in(stream_key, 6), dim), (blocks,), jnp.float32, least / len(pieces), high / len(pieces))
        return jnp.repeat(jnp.exp(draws), shape[dim] // blocks).reshape((-1,) + (1,) * (len(shape) - dim - 1))

    gain = one(*pieces[0])
    for cut in pieces[1:]:
        gain = gain * one(*cut)
    return gain


def bell_draw(stream_key, extent, scale, reach, shards=(), held_as=jnp.bfloat16):
    factor_of = steps_of(stream_key, extent, shards, -0.22, 0.18) if shards else 1.0
    result = jax.random.normal(stream_key, extent, jnp.float32) * scale * factor_of
    return jnp.minimum(jnp.maximum(result, -reach), reach).astype(held_as)


def setup_inputs(seed: int = 0) -> dict:
    key_list = jax.random.split(jax.random.key(seed), 6)
    echoes = bell_draw(key_list[0], (BANDS, 2, PULSES, CELLS), 1.0, 6.0, ((0, 4), (2, 2), (3, 4)))
    range_phase = jnp.clip(jax.random.uniform(key_list[1], (BANDS, CELLS), jnp.float32, -3.140625, 3.140625), -3.140625, 3.140625)
    pulse_shift = place_ends(jax.random.randint(key_list[2], (BANDS, PULSES), -SHIFT_MAX, SHIFT_MAX + 1), jax.random.fold_in(key_list[2], 1), -SHIFT_MAX, SHIFT_MAX).astype(jnp.int32)
    bin_offset = draw_bin_offset(jax.random.fold_in(key_list[5], 71), 0)
    doppler_phase = jnp.clip(jax.random.uniform(key_list[4], (PULSES,), jnp.float32, -3.140625, 3.140625), -3.140625, 3.140625)
    return dict(echoes=echoes, range_phase=range_phase, pulse_shift=pulse_shift, bin_offset=bin_offset, doppler_phase=doppler_phase)


def rotate(values, angles):
    return values * lax.complex(jnp.cos(angles), jnp.sin(angles))


def round_half(values):
    return lax.optimization_barrier(values.astype(jnp.bfloat16)).astype(jnp.float32)


def reference(echoes, range_phase, pulse_shift, bin_offset, doppler_phase):
    pulse_block = math.gcd(PULSES, 512)
    bin_block = math.gcd(COMBINED, 256)
    cell_index = jnp.arange(CELLS, dtype=jnp.int32)

    def range_section(block_id):
        begin_at = (block_id * pulse_block).astype(jnp.int32)
        samples = lax.dynamic_slice_in_dim(echoes, begin_at, pulse_block, 2).astype(jnp.float32)
        shifts = lax.dynamic_slice_in_dim(pulse_shift, begin_at, pulse_block, 1)
        spectrum = jnp.fft.fft(lax.complex(samples[:, 0], samples[:, 1]), axis=-1, norm="ortho")
        spectrum = rotate(spectrum, range_phase[:, None, :])
        ramp = jnp.mod(cell_index[None, None, :] * shifts[:, :, None], CELLS).astype(jnp.float32) * (-2.0 * math.pi / CELLS)
        spectrum = rotate(spectrum, ramp)
        halves = jnp.stack((round_half(jnp.real(spectrum)), round_half(jnp.imag(spectrum))), axis=1)
        frame_sum = jnp.zeros((2, pulse_block, COMBINED + 4 * MARGIN), jnp.float32)
        anchor_zero = jnp.zeros((), jnp.int32)
        for band_id in range(BANDS):
            placed_at = (band_id * OWNED + bin_offset[band_id]).astype(jnp.int32)
            current = lax.dynamic_slice(frame_sum, (anchor_zero, anchor_zero, placed_at), (2, pulse_block, CELLS))
            frame_sum = lax.dynamic_update_slice(frame_sum, current + halves[band_id], (anchor_zero, anchor_zero, placed_at))
        return frame_sum[:, :, 2 * MARGIN: 2 * MARGIN + COMBINED].astype(jnp.bfloat16)

    blocks = lax.map(range_section, jnp.arange(PULSES // pulse_block, dtype=jnp.int32))
    stitched = jnp.transpose(blocks, (3, 1, 0, 2)).reshape(COMBINED, 2, PULSES)

    def azimuth_section(block_id):
        begin_at = (block_id * bin_block).astype(jnp.int32)
        samples = lax.dynamic_slice_in_dim(stitched, begin_at, bin_block, 0).astype(jnp.float32)
        doppler = jnp.fft.fft(lax.complex(samples[:, 0], samples[:, 1]), axis=-1, norm="ortho")
        doppler = rotate(doppler, doppler_phase[None, :])
        focused_block = jnp.fft.ifft(doppler, axis=-1, norm="ortho")
        return jnp.stack((jnp.real(focused_block), jnp.imag(focused_block)), axis=1).astype(jnp.bfloat16)

    focused = lax.map(azimuth_section, jnp.arange(COMBINED // bin_block, dtype=jnp.int32))
    return focused.reshape(COMBINED, 2, PULSES)
```

```python
import functools
import math

import jax
import jax.numpy as jnp
import numpy as np
from jax import lax
from jax.experimental import pallas as pl
from jax.experimental.pallas import tpu as pltpu
from jax.sharding import PartitionSpec as P

MARGIN = 512
SHIFT_MAX = 64
LANES = 128


def shifted(block, axis, distance):
    devices = range(lax.axis_size(axis))
    route = [(i - distance, i) for i in devices if i - distance in devices]
    return lax.ppermute(block, axis, route)


def phases(rows, cols, modulus):
    product = np.arange(rows)[:, None] * np.arange(cols)[None, :] % modulus
    angles = product * (2.0 * np.pi / modulus)
    return np.cos(angles), np.sin(angles)


def high_low(table):
    high = table.astype(jnp.bfloat16)
    low = (table - high.astype(np.float64)).astype(jnp.bfloat16)
    return high, low


def left_table(length, rotation, order_in=None):
    cos, sin = phases(length, length, length)
    sin = rotation * sin
    full = np.block([[cos, -sin], [sin, cos]])
    if order_in is not None:
        full = full[:, order_in]
    return np.concatenate(high_low(full), axis=0)


def right_table(length, rotation):
    cos, sin = phases(length, length, length)
    sin = rotation * sin
    return np.stack(high_low(np.block([[cos, sin], [-sin, cos]])))


def twist_table(rows, length, rotation):
    cos, sin = phases(rows, LANES, length)
    return (np.stack((cos, rotation * sin)) / math.sqrt(length)).astype(np.float32)


def source_order(sources, rows):
    index = np.arange(2 * sources * rows).reshape(2, sources, rows)
    return index.transpose(1, 0, 2).reshape(-1)


def dot(left, right):
    return jnp.dot(left, right, preferred_element_type=jnp.float32)


def rotated(real, imag, by_real, by_imag):
    return real * by_real - imag * by_imag, real * by_imag + imag * by_real


def gathered(ref, index):
    return jnp.concatenate([ref[s, index] for s in range(ref.shape[0])], axis=0)


def range_kernel(shift_ref, x_ref, left_ref, twist_ref, right_ref, turn_ref, o_ref):
    count = x_ref.shape[1]
    outer = twist_ref.shape[1]
    first = pl.program_id(0) * count
    left = left_ref[...]
    highs, lows = [], []
    for g in range(count):
        y = dot(left, gathered(x_ref, g))
        y = y[: 2 * outer] + y[2 * outer :]
        zr, zi = rotated(y[:outer], y[outer:], twist_ref[0], twist_ref[1])
        z = jnp.concatenate((zr, zi), axis=1)
        high = z.astype(jnp.bfloat16)
        highs.append(high)
        lows.append((z - high.astype(jnp.float32)).astype(jnp.bfloat16))
    high = jnp.concatenate(highs, axis=0)
    low = jnp.concatenate(lows, axis=0)
    s = dot(high, right_ref[0]) + dot(low, right_ref[0]) + dot(high, right_ref[1])
    for g in range(count):
        shift = shift_ref[first + g] + SHIFT_MAX
        part = s[g * outer : (g + 1) * outer]
        cr, ci = rotated(part[:, :LANES], part[:, LANES:], turn_ref[shift, 0], turn_ref[shift, 1])
        o_ref[g, 0] = cr.astype(jnp.bfloat16)
        o_ref[g, 1] = ci.astype(jnp.bfloat16)


def azimuth_kernel(
    x_ref, left_ref, twist_ref, right_ref, phase_ref, back_ref, untwist_ref, last_ref, o_ref
):
    count = x_ref.shape[1]
    outer = twist_ref.shape[1]
    left = left_ref[...]
    rows = []
    for g in range(count):
        y = dot(left, gathered(x_ref, g))
        y = y[: 2 * outer] + y[2 * outer :]
        zr, zi = rotated(y[:outer], y[outer:], twist_ref[0], twist_ref[1])
        rows.append(jnp.concatenate((zr, zi), axis=1).astype(jnp.bfloat16))
    z = jnp.concatenate(rows, axis=0)
    d = dot(z, right_ref[0]) + dot(z, right_ref[1])
    rows = []
    for g in range(count):
        part = d[g * outer : (g + 1) * outer]
        dr, di = rotated(part[:, :LANES], part[:, LANES:], phase_ref[0], phase_ref[1])
        rows.append(jnp.concatenate((dr, di), axis=1).astype(jnp.bfloat16))
    z = jnp.concatenate(rows, axis=0)
    d = dot(z, back_ref[0]) + dot(z, back_ref[1])
    last = last_ref[...]
    for g in range(count):
        part = d[g * outer : (g + 1) * outer]
        er, ei = rotated(part[:, :LANES], part[:, LANES:], untwist_ref[0], untwist_ref[1])
        e = jnp.concatenate((er, ei), axis=0).astype(jnp.bfloat16)
        y = dot(last, e)
        y = y[: 2 * outer] + y[2 * outer :]
        o_ref[g, 0] = y[:outer].astype(jnp.bfloat16)
        o_ref[g, 1] = y[outer:].astype(jnp.bfloat16)


def whole_spec(array):
    return pl.BlockSpec(array.shape, lambda i, *_: (0,) * array.ndim)


def run(kernel, name, tables, x, outer, block, scalars=()):
    sources, total, rows, _ = x.shape
    block = math.gcd(block, total)
    grid_spec = pltpu.PrefetchScalarGridSpec(
        num_scalar_prefetch=len(scalars),
        grid=(total // block,),
        in_specs=[pl.BlockSpec((sources, block, rows, LANES), lambda i, *_: (0, i, 0, 0))]
        + [whole_spec(t) for t in tables],
        out_specs=pl.BlockSpec((block, 2, outer, LANES), lambda i, *_: (i, 0, 0, 0)),
    )
    elements = total * outer * LANES
    return pl.pallas_call(
        kernel,
        grid_spec=grid_spec,
        out_shape=jax.ShapeDtypeStruct((total, 2, outer, LANES), jnp.bfloat16),
        compiler_params=pltpu.CompilerParams(vmem_limit_bytes=48 * 1024 * 1024),
        cost_estimate=pl.CostEstimate(
            flops=elements * 4096, bytes_accessed=elements * 8, transcendentals=0
        ),
        name=name,
    )(*scalars, x, *tables)


def packed_rows(x):
    sources, total, rows, lanes = x.shape
    if rows % 16 == 0:
        return x
    return x.transpose(1, 0, 2, 3).reshape(1, total, sources * rows, lanes)


def body(echoes, range_phase, pulse_shift, bin_offset, doppler_phase):
    range_count = lax.axis_size("range")
    pulse_count = lax.axis_size("pulse")
    group_size = pulse_count * range_count
    band_rows = echoes.shape[2]
    cells_local = echoes.shape[3]
    n_local = band_rows // range_count
    cell_count = cells_local * range_count
    owned_bins = cell_count - 2 * MARGIN
    spill_len = 2 * MARGIN
    pulses = band_rows * pulse_count

    outer = cell_count // LANES
    part_rows = cells_local // LANES
    rows_in = echoes[0].reshape(2, range_count, n_local, part_rows, LANES)
    rows_in = rows_in.transpose(1, 2, 0, 3, 4).reshape(range_count, n_local, 2 * part_rows, LANES)
    received = lax.all_to_all(rows_in, "range", split_axis=0, concat_axis=0, tiled=True)
    shifts = jnp.arange(-SHIFT_MAX, SHIFT_MAX + 1, dtype=jnp.int32)
    cell_index = (
        jnp.arange(outer, dtype=jnp.int32)[:, None]
        + outer * jnp.arange(LANES, dtype=jnp.int32)[None, :]
    )
    angles = jnp.mod(cell_index[None] * shifts[:, None, None], cell_count).astype(jnp.float32) * (
        -2.0 * math.pi / cell_count
    )
    filter_phase = range_phase[0].reshape(LANES, outer).T
    turn_real, turn_imag = rotated(
        jnp.cos(angles), jnp.sin(angles), jnp.cos(filter_phase), jnp.sin(filter_phase)
    )
    tables = [
        jnp.asarray(left_table(outer, -1.0, source_order(range_count, part_rows))),
        jnp.asarray(twist_table(outer, cell_count, -1.0)),
        jnp.asarray(right_table(LANES, -1.0)),
        jnp.stack((turn_real, turn_imag), axis=1),
    ]
    spectrum = run(
        range_kernel, "range", tables, packed_rows(received), outer, 16, (pulse_shift[0],)
    )
    fold = n_local // LANES
    contrib = spectrum.reshape(fold, LANES, 2, outer, LANES).transpose(4, 3, 2, 0, 1)
    contrib = contrib.reshape(cell_count, 2 * fold, LANES)

    band_index = lax.axis_index("band")
    offset = jnp.sum(
        jnp.where(jnp.arange(bin_offset.shape[0], dtype=jnp.int32) == band_index, bin_offset, 0)
    )
    padded = jnp.pad(contrib, ((spill_len, spill_len), (0, 0), (0, 0)))
    upper = lax.dynamic_slice_in_dim(padded, owned_bins + 2 * spill_len - offset, spill_len, 0)
    lower = lax.dynamic_slice_in_dim(padded, spill_len - offset, spill_len, 0)
    from_below = shifted(upper, "band", 1)
    from_above = shifted(lower, "band", -1)
    own = lax.dynamic_slice_in_dim(padded, 2 * spill_len - offset, owned_bins, 0)
    rest = ((0, 0), (0, 0))
    stitched = (
        own.astype(jnp.float32)
        + jnp.pad(from_below, ((0, owned_bins - spill_len),) + rest).astype(jnp.float32)
        + jnp.pad(from_above, ((owned_bins - spill_len, 0),) + rest).astype(jnp.float32)
    ).astype(jnp.bfloat16)

    bins_local = owned_bins // group_size
    outer = pulses // LANES
    blocks = stitched.reshape(group_size, bins_local, 2 * fold, LANES)
    samples = lax.all_to_all(blocks, ("pulse", "range"), split_axis=0, concat_axis=0, tiled=True)
    doppler = doppler_phase.reshape(LANES, outer).T
    tables = [
        jnp.asarray(left_table(outer, -1.0, source_order(group_size, fold))),
        jnp.asarray(twist_table(outer, pulses, -1.0)),
        jnp.asarray(right_table(LANES, -1.0)),
        jnp.stack((jnp.cos(doppler), jnp.sin(doppler))),
        jnp.asarray(right_table(LANES, 1.0)),
        jnp.asarray(twist_table(outer, pulses, 1.0)),
        jnp.asarray(left_table(outer, 1.0)),
    ]
    focused = run(azimuth_kernel, "azimuth", tables, packed_rows(samples), outer, 8)
    return focused.reshape(bins_local, 2, pulses)


def solution(mesh):
    in_specs = (
        P("band", None, "pulse", "range"),
        P("band", None),
        P("band", ("pulse", "range")),
        P(),
        P(),
    )
    out_specs = P(("band", "pulse", "range"), None, None)
    return jax.shard_map(body, mesh=mesh, in_specs=in_specs, out_specs=out_specs, check_vma=False)
```
